32 devices in a mesh: dp: 8 (over z, y), tensor: 4 (over x, core).
Axes of the slice: x: 2, y: 2, z: 4, core: 2. Of those that a mesh axis runs over, the one named last changes fastest.
Arguments:
- tokens: bfloat16 [4096, 768], P(('dp', 'tensor')), may hold values from -6 to 6
- cotangent: bfloat16 [4096, 768], P(('dp', 'tensor')), may hold values from -6 to 6
- selected: int32 [4096], P(('dp', 'tensor')), may hold values from 0 to 1, as said below
- buckets: int32 [1023], replicated, may hold values from 0 to 511, as said below
- projector: bfloat16 [3, 768, 768], P(None, 'dp', 'tensor'), may hold values from -0.21875 to 0.21875
- intercepts: bfloat16 [3, 768], P(None, 'tensor')
- combiner: bfloat16 [768, 768], P('dp', 'tensor'), may hold values from -2 to 2
- offset: bfloat16 [768], replicated, may hold values from -1.1953125 to 1.1953125
- relative: bfloat16 [512, 768], replicated, may hold values from -6 to 6
- stretch: float32 [768], replicated, may hold values from 0.5 to 1.5
- uplift: float32 [768], replicated, may hold values from -1.2 to 1.2
- expander: bfloat16 [768, 3072], P(None, 'tensor'), may hold values from -0.21875 to 0.21875
- threshold: bfloat16 [3072], P('tensor'), may hold values from -3 to 3
- reducer: bfloat16 [3072, 768], P('tensor'), may hold values from -0.109375 to 0.109375
- residue: bfloat16 [768], replicated, may hold values from -1.1953125 to 1.1953125
- amplify: float32 [768], replicated, may hold values from 0.5 to 1.5
- displace: float32 [768], replicated, may hold values from -1.2 to 1.2
Outputs:
- result: bfloat16 [4096, 768], P(('dp', 'tensor'))
- tokens_grad: float32 [4096, 768], P(('dp', 'tensor'))
- projector_grad: float32 [3, 768, 768], P(None, 'dp', 'tensor')
- intercepts_grad: float32 [3, 768], P(None, 'tensor')
- combiner_grad: float32 [768, 768], P('dp', 'tensor')
- offset_grad: float32 [768], replicated
- relative_grad: float32 [512, 768], replicated
- stretch_grad: float32 [768], replicated
- uplift_grad: float32 [768], replicated
- expander_grad: float32 [768, 3072], P(None, 'tensor')
- threshold_grad: float32 [3072], P('tensor')
- reducer_grad: float32 [3072, 768], P('tensor')
- residue_grad: float32 [768], replicated
- amplify_grad: float32 [768], replicated
- displace_grad: float32 [768], replicated
The draws below stay inside these ranges and needn't reach their ends.
Inputs may be any that keep to these rules, and one draw needn't show every extreme that they name: buckets[d + 511] is the bucket of relative offset d. Each aligned quarter of a sequence (128 tokens) has the same number of selected tokens as the other quarters of its sequence, at least 1 and at most 51; in every draw all sequences of some aligned run of 1 sequence have that most in each quarter.
All inputs are finite; a program needn't handle non-finite values.
Results may differ from the reference program's by a relative error of at most 0.019.
Values may be sent and summed in bfloat16 or wider, within the bound.
A program may use at most 128 MiB of HBM per device.

```python
import math
import jax
import jax.numpy as jnp
from jax import lax

D = 768
HEADS = 12
FF = 3072
SPAN = 256
SEQ_LEN = 512
SEQ_DEV = 1
HEAD_DIM = 64
TOKENS = 4096


def draw_buckets(key, part):
    offsets = jnp.arange(2 * SEQ_LEN - 1, dtype=jnp.int32) - (SEQ_LEN - 1)
    jitter = jax.random.randint(key, offsets.shape, -3, 4, dtype=jnp.int32)
    moved = jnp.where(jnp.abs(offsets) >= 8, offsets + jitter, offsets)
    return (jnp.clip(moved, -SPAN, SPAN - 1) + SPAN).astype(jnp.int32)


def draw_selected(key, part):
    count = TOKENS // SEQ_LEN
    quarter = SEQ_LEN // 4
    most = quarter * 2 // 5
    least = max(1, (quarter + 19) // 20)
    picks = jax.random.randint(jax.random.fold_in(key, 1), (count,), least, most + 1, dtype=jnp.int32)
    groups = count // SEQ_DEV
    chosen = jax.random.randint(jax.random.fold_in(key, 3), (), 0, groups, dtype=jnp.int32)
    owner = jnp.arange(count, dtype=jnp.int32) // SEQ_DEV
    picks = jnp.where(owner == chosen, most, picks).astype(jnp.int32)
    seeds = jax.random.split(jax.random.fold_in(key, 2), count * 4)
    ranks = jax.vmap(lambda k: jax.random.permutation(k, quarter))(seeds).astype(jnp.int32)
    ranks = ranks.reshape(count, 4, quarter)
    return (ranks < picks[:, None, None]).astype(jnp.int32).reshape(TOKENS)


def draw_intercepts(key, part):
    base = jax.random.normal(key, (3, D), jnp.float32)
    scales = jnp.array([0.5, 0.5, 0.02], jnp.float32)
    return (base * scales[:, None]).astype(jnp.bfloat16)


def block_scale(key, dims, pieces, low, largest):
    loudness = 1.0
    for position, shards_of in pieces:
        steps = jax.random.uniform(jax.random.fold_in(jax.random.fold_in(key, 6), position), (shards_of,), jnp.float32, low / len(pieces), largest / len(pieces))
        loudness = loudness * jnp.repeat(jnp.exp(steps), dims[position] // shards_of).reshape((-1,) + (1,) * (len(dims) - 1 - position))
    return loudness


def normal_values(rng, dims, deviation, most, shards=(), kind=jnp.bfloat16):
    result = deviation * jax.random.normal(rng, dims, jnp.float32)
    if shards:
        result = result * block_scale(rng, dims, shards, -0.22, 0.18)
    return jnp.clip(result, -most, most).astype(kind)


def setup_inputs(seed: int = 0) -> dict:
    splits = jax.random.split(jax.random.key(seed), 18)
    return {
        "tokens": normal_values(splits[0], (TOKENS, D), 1.0, 6.0, ((0, 32),)),
        "cotangent": normal_values(splits[1], (TOKENS, D), 1.0, 6.0, ((0, 32),)),
        "selected": draw_selected(jax.random.fold_in(splits[17], 71), 0),
        "buckets": draw_buckets(jax.random.fold_in(splits[17], 71), 0),
        "projector": normal_values(splits[4], (3, D, D), D ** -0.5, 0.21875, ((1, 8), (2, 4))),
        "intercepts": draw_intercepts(jax.random.fold_in(splits[17], 71), 0),
        "combiner": normal_values(splits[6], (D, D), 8 ** -0.5, 2.0, ((0, 8), (1, 4))),
        "offset": normal_values(splits[7], (D,), 0.2, 1.1953125),
        "relative": normal_values(splits[8], (2 * SPAN, D), 1.0, 6.0),
        "stretch": jnp.clip(1.0 + 0.1 * jax.random.normal(splits[9], (D,), jnp.float32), 0.5, 1.5),
        "uplift": normal_values(splits[10], (D,), 0.2, 1.2, (), jnp.float32),
        "expander": normal_values(splits[11], (D, FF), D ** -0.5, 0.21875, ((1, 4),)),
        "threshold": normal_values(splits[12], (FF,), 0.5, 3.0, ((0, 4),)),
        "reducer": normal_values(splits[13], (FF, D), FF ** -0.5, 0.109375, ((0, 4),)),
        "residue": normal_values(splits[14], (D,), 0.2, 1.1953125),
        "amplify": jnp.clip(1.0 + 0.1 * jax.random.normal(splits[15], (D,), jnp.float32), 0.5, 1.5),
        "displace": normal_values(splits[16], (D,), 0.2, 1.2, (), jnp.float32),
    }


@jax.custom_vjp
def low(v):
    return lax.optimization_barrier(v.astype(jnp.bfloat16)).astype(jnp.float32)

@jax.custom_vjp
def lower_backward(v):
    return v

def low_keep(v):
    return (low(v), None)

def low_pass(kept, grad):
    return (grad,)

def back_keep(v):
    return (v, None)

def back_low(kept, grad):
    return (low(grad),)
low.defvjp(low_keep, low_pass)
lower_backward.defvjp(back_keep, back_low)
FULL_ACCURACY = lax.Precision.HIGHEST

def layer_norm(value, gain, shift):
    mean = lax.optimization_barrier(jnp.mean(value, -1, keepdims=True))
    center = value - mean
    variance = lax.optimization_barrier(jnp.mean(center * center, -1, keepdims=True))
    return center * lax.rsqrt(variance + 1e-05) * gain + shift

def attend(queries, keys, values, relative_position_key, pos_query, index):
    length = queries.shape[0]
    query_head_split = queries.reshape(length, HEADS, HEAD_DIM)
    key_heads = keys.reshape(length, HEADS, HEAD_DIM)
    value_heads = values.reshape(length, HEADS, HEAD_DIM)
    position_key_heads = relative_position_key.reshape(-1, HEADS, HEAD_DIM)
    pos_query_heads = pos_query.reshape(-1, HEADS, HEAD_DIM)
    direct = jnp.einsum('ihd,jhd->hij', query_head_split, key_heads, precision=FULL_ACCURACY)
    nearby_unscaled = lower_backward(jnp.einsum('loq,goq->olg', query_head_split, position_key_heads, precision=FULL_ACCURACY))
    far_raw = lower_backward(jnp.einsum('jhd,bhd->hjb', key_heads, pos_query_heads, precision=FULL_ACCURACY))
    full = jnp.broadcast_to(index[None], direct.shape)
    near = jnp.take_along_axis(nearby_unscaled, full, axis=2)
    far = jnp.swapaxes(jnp.take_along_axis(far_raw, full, axis=2), 1, 2)
    scores = lower_backward((direct + near + far) * (1.0 / math.sqrt(3 * HEAD_DIM)))
    probs = jax.nn.softmax(scores, axis=-1)
    context = jnp.einsum('hij,jhd->ihd', low(probs), value_heads, precision=FULL_ACCURACY)
    return context.reshape(length, D)

def layer(block, params, index):
    projector, intercepts, combiner, offset, relative, stretch, uplift, expander, threshold, reducer, residue, amplify, displace = params
    count = block.shape[0] // SEQ_LEN
    mixed = jnp.einsum('ti,mic->mtc', block, projector, precision=FULL_ACCURACY) + intercepts[:, None, :]
    queries = lower_backward(low(mixed[0]))
    keys = lower_backward(low(mixed[1]))
    values = lower_backward(low(mixed[2]))
    pos_query = low(jnp.dot(relative, projector[0], precision=FULL_ACCURACY) + intercepts[0])
    relative_position_key = low(jnp.dot(relative, projector[1], precision=FULL_ACCURACY) + intercepts[1])

    def one(item):
        return attend(item[0], item[1], item[2], relative_position_key, pos_query, index)
    context = lax.map(jax.checkpoint(one), (queries.reshape(count, SEQ_LEN, D), keys.reshape(count, SEQ_LEN, D), values.reshape(count, SEQ_LEN, D)))
    context = lower_backward(low(context.reshape(-1, D)))
    attended = lower_backward(jnp.dot(context, combiner.T, precision=FULL_ACCURACY) + offset)
    mid = layer_norm(block + attended, stretch, uplift)
    inner = lower_backward(jnp.dot(low(mid), expander, precision=FULL_ACCURACY) + threshold)
    active = low(jax.nn.gelu(inner, approximate=False))
    outer = lower_backward(jnp.dot(active, reducer, precision=FULL_ACCURACY) + residue)
    return layer_norm(mid + outer, amplify, displace)

def reference(tokens, cotangent, selected, buckets, projector, intercepts, combiner, offset, relative, stretch, uplift, expander, threshold, reducer, residue, amplify, displace):
    places = jnp.arange(SEQ_LEN, dtype=jnp.int32)
    index = jnp.take(buckets, places[:, None] - places[None, :] + (SEQ_LEN - 1)).astype(jnp.int32)
    params = tuple((p.astype(jnp.float32) for p in (projector, intercepts, combiner, offset, relative, stretch, uplift, expander, threshold, reducer, residue, amplify, displace)))
    sequences = TOKENS // SEQ_LEN
    per_block = math.gcd(sequences, max(1, 4096 // SEQ_LEN))
    blocks = sequences // per_block
    inputs = tokens.astype(jnp.float32).reshape(blocks, per_block * SEQ_LEN, D)
    upstream = (cotangent.astype(jnp.float32) * selected.astype(jnp.float32)[:, None]).reshape(blocks, per_block * SEQ_LEN, D)

    def step(total, item):
        block, grad_block = item
        output, pull = jax.vjp(lambda x, *p: layer(x, p, index), block, *params)
        grads = pull(grad_block)
        total = jax.tree.map(lambda a, b: a + b, total, tuple(grads[1:]))
        return (total, (output.astype(jnp.bfloat16), grads[0]))
    zeros = tuple((jnp.zeros(p.shape, jnp.float32) for p in params))
    total, (outputs, input_grads) = lax.scan(step, zeros, (inputs, upstream))
    return (outputs.reshape(TOKENS, D), input_grads.reshape(TOKENS, D), total[0], total[1], total[2], total[3], total[4], total[5], total[6], total[7], total[8], total[9], total[10], total[11], total[12])
```

```python
import functools
import math

import jax, jax.numpy as jnp
from jax import lax
from jax.experimental import pallas as pl
from jax.experimental.pallas import tpu as pltpu
from jax.sharding import PartitionSpec as P

HEAD_DIM = 64
BLK = 128
F32, BF16 = jnp.float32, jnp.bfloat16

def nn(a, b):
    return lax.dot_general(a, b, (((1,), (0,)), ((), ())), preferred_element_type=F32)

def nt(a, b):
    return lax.dot_general(a, b, (((1,), (1,)), ((), ())), preferred_element_type=F32)

def tn(a, b):
    return lax.dot_general(a, b, (((0,), (0,)), ((), ())), preferred_element_type=F32)

def attn_fwd_kernel(scale, x_ref, w_ref, bias_ref, rel_ref, bcol_ref,
                    probs_ref, mixed_ref, table_ref, ctx_ref, part_ref, far_ref, acc_ref):
    length = x_ref.shape[0]
    cols = ctx_ref.shape[1]
    classes = rel_ref.shape[0]
    span = table_ref.shape[0]
    blocks = length // BLK
    win = length + BLK
    bias = bias_ref[...].astype(F32)
    mixed_ref[...] = (nn(x_ref[...], w_ref[:, : 3 * cols]) + bias).astype(BF16)
    pos = (nn(rel_ref[...], w_ref[:, : 2 * cols]) + bias[:, : 2 * cols]).astype(BF16)
    spread = (bcol_ref[...] == lax.broadcasted_iota(jnp.int32, (span, classes), 1)).astype(BF16)
    table_ref[...] = nn(spread, pos).astype(BF16)
    lanes = lax.broadcasted_iota(jnp.int32, (1, cols), 1) // HEAD_DIM
    acc_ref[...] = jnp.zeros_like(acc_ref)

    def head(h, carry):
        own = lanes == h
        pick = lambda v: jnp.where(own, v, jnp.zeros_like(v))
        key_h = pick(mixed_ref[:, cols : 2 * cols])
        for b in range(blocks):
            start = length - BLK * (b + 1)
            rows = slice(BLK * b, BLK * (b + 1))
            wide = nt(key_h[rows], table_ref[start : start + win, :cols])
            turned = pltpu.roll(wide, win - BLK + 1, 1, stride=1, stride_axis=0)[:, :length]
            far_ref[:, rows] = turned.T
        value_h = pick(mixed_ref[:, 2 * cols : 3 * cols])
        for b in range(blocks):
            start = length - BLK * (b + 1)
            rows = slice(BLK * b, BLK * (b + 1))
            query = pick(mixed_ref[rows, :cols])
            wide = nt(query, table_ref[start : start + win, cols : 2 * cols])
            near = pltpu.roll(wide, win - BLK + 1, 1, stride=1, stride_axis=0)[:, :length]
            scores = (nt(query, key_h) + near + far_ref[rows, :]) * scale
            top = jnp.max(scores, -1, keepdims=True)
            weights = jnp.exp(scores - top)
            probs = weights / jnp.sum(weights, -1, keepdims=True)
            probs_ref[h, rows, :] = probs
            acc_ref[rows, :] += nn(probs.astype(BF16), value_h)
        return carry

    lax.fori_loop(0, cols // HEAD_DIM, head, 0)
    ctx_ref[...] = acc_ref[...].astype(BF16)
    part_ref[...] = nt(ctx_ref[...], w_ref[:, 3 * cols :]).astype(BF16)

def attn_fwd(x, w, bias, rel, bcol):
    length = x.shape[0]
    cols = w.shape[1] // 4
    width = w.shape[0]
    scale = 1.0 / math.sqrt(3 * HEAD_DIM)
    heads = cols // HEAD_DIM
    span = bcol.shape[0]
    S = jax.ShapeDtypeStruct
    return pl.pallas_call(
        functools.partial(attn_fwd_kernel, scale),
        out_shape=(S((heads, length, length), F32), S((length, 3 * cols), BF16), S((span, 2 * cols), BF16),
                   S((length, cols), BF16), S((length, width), BF16)),
        scratch_shapes=[pltpu.VMEM((length, length), F32), pltpu.VMEM((length, cols), F32)],
        name="attn_fwd",
    )(x, w, bias, rel, bcol)

def attn_bwd_kernel(scale, x_ref, w_ref, rel_ref, bcol_ref, probs_ref, mixed_ref, table_ref, ctx_ref, rows_ref, sel_ref,
                    grads_ref, part_ref, relpart_ref, bias_ref,
                    dctx_ref, dctx_t, turn_t, dq_ref, dk_ref, dv_t, dpos_t, ds_ref):
    length = x_ref.shape[0]
    cols = ctx_ref.shape[1]
    classes = rel_ref.shape[0]
    span = table_ref.shape[0]
    blocks = length // BLK
    win = length + BLK
    keep = sel_ref.shape[0] // blocks
    flip = (lax.broadcasted_iota(jnp.int32, (BLK, BLK), 0) + lax.broadcasted_iota(jnp.int32, (BLK, BLK), 1) == BLK - 1).astype(BF16)
    small = nn(rows_ref[...], w_ref[:, 3 * cols :]).astype(BF16)
    ctx_small = []
    for b in range(blocks):
        rows = slice(BLK * b, BLK * (b + 1))
        few = slice(keep * b, keep * (b + 1))
        dctx_ref[rows, :] = tn(sel_ref[few, :], small[few]).astype(BF16)
        ctx_small.append(nn(sel_ref[few, :], ctx_ref[rows, :]).astype(BF16))
        turn_t[:cols, rows] = tn(mixed_ref[rows, :cols], flip).astype(BF16)
        turn_t[cols:, rows] = tn(mixed_ref[rows, cols : 2 * cols], flip).astype(BF16)
    dctx_t[...] = dctx_ref[...].T
    grads_ref[:, 3 * cols :] = tn(rows_ref[...], jnp.concatenate(ctx_small, 0)).astype(BF16)
    lanes = lax.broadcasted_iota(jnp.int32, (1, cols), 1) // HEAD_DIM
    dq_ref[...] = jnp.zeros_like(dq_ref)
    dk_ref[...] = jnp.zeros_like(dk_ref)
    dpos_t[...] = jnp.zeros_like(dpos_t)
    blank = jnp.zeros((BLK, BLK), F32)

    def head(h, carry):
        own = lanes == h
        pick = lambda v: jnp.where(own, v, jnp.zeros_like(v))
        mine = pl.ds(pl.multiple_of(h * HEAD_DIM, HEAD_DIM), HEAD_DIM)
        key_h = pick(mixed_ref[:, cols : 2 * cols])
        query_h = pick(mixed_ref[:, :cols])
        value = mixed_ref[:, 2 * cols : 3 * cols]
        posq_h = pick(table_ref[:, :cols])
        posk_h = pick(table_ref[:, cols : 2 * cols])
        total = jnp.zeros((HEAD_DIM, length), F32)
        for b in range(blocks):
            start = length - BLK * (b + 1)
            rows = slice(BLK * b, BLK * (b + 1))
            probs = probs_ref[h, rows, :]
            dprobs = nt(pick(dctx_ref[rows, :]), value)
            dscores = (probs * (dprobs - jnp.sum(probs * dprobs, -1, keepdims=True))).astype(BF16)
            ds_ref[rows, :] = dscores
            total += nn(dctx_t[mine, rows], probs.astype(BF16))
            turned = nn(flip, dscores)
            moved = pltpu.roll(jnp.concatenate([turned, blank], 1), 0, 1, stride=1, stride_axis=0).astype(BF16)
            dq_ref[rows, :] += nn(turned.astype(BF16), key_h) + nn(moved, posk_h[start : start + win])
            low = pl.ds(pl.multiple_of(cols + h * HEAD_DIM, HEAD_DIM), HEAD_DIM)
            dpos_t[low, start : start + win] += nn(turn_t[mine, rows], moved)
        dv_t[mine, :] = total
        for b in range(blocks):
            start = length - BLK * (b + 1)
            rows = slice(BLK * b, BLK * (b + 1))
            turned = nt(flip, ds_ref[:, rows])
            moved = pltpu.roll(jnp.concatenate([turned, blank], 1), 0, 1, stride=1, stride_axis=0).astype(BF16)
            dk_ref[rows, :] += nn(turned.astype(BF16), query_h) + nn(moved, posq_h[start : start + win])
            low = pl.ds(pl.multiple_of(cols + h * HEAD_DIM, HEAD_DIM), HEAD_DIM)
            dpos_t[mine, start : start + win] += nn(turn_t[low, rows], moved)
        return carry

    lax.fori_loop(0, cols // HEAD_DIM, head, 0)
    order = lambda ref: jnp.concatenate([nn(flip, (ref[BLK * b : BLK * (b + 1), :] * scale).astype(BF16)).astype(BF16) for b in range(blocks)], 0)
    dmixed = jnp.concatenate([order(dq_ref), order(dk_ref), dv_t[...].T.astype(BF16)], 1)
    spread = (bcol_ref[...] == lax.broadcasted_iota(jnp.int32, (span, classes), 1)).astype(BF16)
    wide = dpos_t[...] * scale
    high = wide.astype(BF16)
    dpos = (nn(high, spread) + nn((wide - high.astype(F32)).astype(BF16), spread)).T
    dpos_low = dpos.astype(BF16)
    sums = jnp.sum(dmixed.astype(F32), 0, keepdims=True)
    bias_ref[...] = sums
    bias_ref[:, : 2 * cols] += jnp.sum(dpos, 0, keepdims=True)
    relpart_ref[...] = nt(dpos_low, w_ref[:, : 2 * cols]).astype(BF16)
    part_ref[...] = nt(dmixed, w_ref[:, : 3 * cols]).astype(BF16)
    both = tn(x_ref[...], dmixed)
    grads_ref[:, : 2 * cols] = (both[:, : 2 * cols] + tn(rel_ref[...], dpos_low)).astype(BF16)
    grads_ref[:, 2 * cols : 3 * cols] = both[:, 2 * cols :].astype(BF16)

def attn_bwd(x, w, rel, bcol, probs, mixed, table, ctx, rows, sel):
    length, width = x.shape
    cols = w.shape[1] // 4
    scale = 1.0 / math.sqrt(3 * HEAD_DIM)
    span = bcol.shape[0]
    S = jax.ShapeDtypeStruct
    V = pltpu.VMEM
    return pl.pallas_call(
        functools.partial(attn_bwd_kernel, scale),
        out_shape=(S((width, 4 * cols), BF16), S((length, width), BF16), S((rel.shape[0], width), BF16), S((1, 3 * cols), F32)),
        scratch_shapes=[V((length, cols), BF16), V((cols, length), BF16), V((2 * cols, length), BF16), V((length, cols), F32), V((length, cols), F32),
                        V((cols, length), F32), V((2 * cols, span), F32), V((length, length), BF16)],
        name="attn_bwd",
    )(x, w, rel, bcol, probs, mixed, table, ctx, rows, sel)


EPSILON = 1e-05


def normalize(value, gain, shift):
    mean = jnp.mean(value, -1, keepdims=True)
    center = value - mean
    inverse = lax.rsqrt(jnp.mean(center * center, -1, keepdims=True) + EPSILON)
    unit = center * inverse
    return (unit * gain + shift, unit, inverse)


def normalize_back(incoming, gain, unit, inverse):
    scaled = incoming * gain
    result = inverse * (
        scaled
        - jnp.mean(scaled, -1, keepdims=True)
        - unit * jnp.mean(scaled * unit, -1, keepdims=True)
    )
    return (result, jnp.sum(incoming * unit, 0), jnp.sum(incoming, 0))


def cumulative(inner):
    return 0.5 * (1.0 + lax.erf(inner * (1.0 / math.sqrt(2.0))))


def shards(tokens, cotangent, selected, buckets, projector, intercepts, combiner, offset, relative, stretch, uplift,
           expander, threshold, reducer, residue, amplify, displace):
    quarter, width = tokens.shape
    cols = projector.shape[2]
    group = lax.axis_size("tensor")
    keep = -(-(quarter * 2 // 5) // 16) * 16
    x = lax.all_gather(tokens, "tensor", axis=0, tiled=True)
    packed = jnp.concatenate([projector[0], projector[1], projector[2], combiner], 1)
    w = lax.all_gather(packed, "dp", axis=0, tiled=True)
    chosen = lax.all_gather(selected, "tensor", axis=0, tiled=True).reshape(group, quarter)
    rank = jnp.cumsum(chosen, 1) - 1
    sel = ((rank[:, None, :] == jnp.arange(keep, dtype=jnp.int32)[None, :, None]) & (chosen[:, None, :] == 1)).astype(BF16)
    mine = lax.dynamic_index_in_dim(sel, lax.axis_index("tensor"), 0, keepdims=False)
    sel_flat = sel.reshape(group * keep, quarter)
    bias = intercepts.reshape(1, 3 * cols)
    span = buckets.shape[0] + 1
    bcol = jnp.concatenate([buckets[::-1], jnp.full((1,), -1, jnp.int32)]).reshape(span, 1)
    probs, mixed, table, ctx, part = attn_fwd(x, w, bias, relative, bcol)
    attended = lax.psum_scatter(part, "tensor", scatter_dimension=0, tiled=True).astype(F32) + offset.astype(F32)
    mid, mid_unit, mid_inverse = normalize(tokens.astype(F32) + attended, stretch, uplift)
    hidden_in = lax.all_gather(mid.astype(BF16), "tensor", axis=0, tiled=True)
    bent = threshold.astype(F32)
    inner = nn(hidden_in, expander) + bent
    active = (inner * cumulative(inner)).astype(BF16)
    feed = nn(active, reducer).astype(BF16)
    outer = lax.psum_scatter(feed, "tensor", scatter_dimension=0, tiled=True).astype(F32) + residue.astype(F32)
    final, end_unit, end_inverse = normalize(mid + outer, amplify, displace)
    upstream = cotangent.astype(F32) * selected.astype(F32)[:, None]
    d_end, amplify_part, displace_part = normalize_back(upstream, amplify, end_unit, end_inverse)
    d_outer = d_end.astype(BF16)
    residue_part = jnp.sum(d_outer.astype(F32), 0)
    d_rows = lax.all_gather(nn(mine, d_outer).astype(BF16), "tensor", axis=0, tiled=True)
    few = lax.dot_general(sel, hidden_in.reshape(group, quarter, width), (((2,), (1,)), ((0,), (0,))), preferred_element_type=F32)
    few = few.astype(BF16).reshape(group * keep, width)
    inner_few = nn(few, expander) + bent
    weight = cumulative(inner_few)
    active_few = (inner_few * weight).astype(BF16)
    slope = weight + inner_few * jnp.exp(-0.5 * inner_few * inner_few) * (1.0 / math.sqrt(2.0 * math.pi))
    d_inner = (nt(d_rows, reducer) * slope).astype(BF16)
    reducer_part = tn(active_few, d_rows).astype(BF16)
    expander_part = tn(few, d_inner).astype(BF16)
    threshold_part = jnp.sum(d_inner.astype(F32), 0)
    back = nt(d_inner, expander).astype(BF16)
    d_feed_few = lax.psum_scatter(back, "tensor", scatter_dimension=0, tiled=True)
    d_feed = tn(mine, d_feed_few)
    d_mid, stretch_part, uplift_part = normalize_back(d_end + d_feed, stretch, mid_unit, mid_inverse)
    d_attended = d_mid.astype(BF16)
    offset_part = jnp.sum(d_attended.astype(F32), 0)
    d_attn = lax.all_gather(nn(mine, d_attended).astype(BF16), "tensor", axis=0, tiled=True)
    grads, input_part, rel_part, bias_part = attn_bwd(x, w, relative, bcol, probs, mixed, table, ctx, d_attn, sel_flat)
    tokens_grad = d_mid + lax.psum_scatter(input_part, "tensor", scatter_dimension=0, tiled=True).astype(F32)
    mine_grads = lax.psum_scatter(grads, "dp", scatter_dimension=0, tiled=True).astype(F32)
    projector_grad = jnp.stack([mine_grads[:, :cols], mine_grads[:, cols : 2 * cols], mine_grads[:, 2 * cols : 3 * cols]])
    combiner_grad = mine_grads[:, 3 * cols :]
    expander_grad, reducer_grad = lax.psum((expander_part, reducer_part), "dp")
    threshold_grad, intercepts_grad = lax.psum((threshold_part, bias_part.reshape(3, cols)), "dp")
    small = jnp.stack([stretch_part, uplift_part, amplify_part, displace_part, offset_part, residue_part])
    small = lax.psum(small, ("dp", "tensor"))
    relative_grad = lax.psum(rel_part, ("dp", "tensor")).astype(F32)
    return (final.astype(BF16), tokens_grad, projector_grad, intercepts_grad, combiner_grad, small[4], relative_grad,
            small[0], small[1], expander_grad.astype(F32), threshold_grad, reducer_grad.astype(F32), small[5], small[2], small[3])


def solution(mesh):
    both = P(("dp", "tensor"), None)
    return jax.shard_map(
        shards,
        mesh=mesh,
        in_specs=(both, both, P(("dp", "tensor")), P(), P(None, "dp", "tensor"), P(None, "tensor"), P("dp", "tensor"), P(), P(), P(), P(),
                  P(None, "tensor"), P("tensor"), P("tensor", None), P(), P(), P()),
        out_specs=(both, both, P(None, "dp", "tensor"), P(None, "tensor"), P("dp", "tensor"), P(), P(), P(), P(),
                   P(None, "tensor"), P("tensor"), P("tensor", None), P(), P(), P()),
        check_vma=False,
    )
```

```python
import functools
import math

import jax, jax.numpy as jnp
from jax import lax
from jax.experimental import pallas as pl
from jax.experimental.pallas import tpu as pltpu
from jax.sharding import PartitionSpec as P

HEAD_DIM = 64
BLK = 128
EPSILON = 1e-05
F32, BF16 = jnp.float32, jnp.bfloat16

def nn(a, b):
    return lax.dot_general(a, b, (((1,), (0,)), ((), ())), preferred_element_type=F32)

def nt(a, b):
    return lax.dot_general(a, b, (((1,), (1,)), ((), ())), preferred_element_type=F32)

def tn(a, b):
    return lax.dot_general(a, b, (((0,), (0,)), ((), ())), preferred_element_type=F32)

def attn_fwd_kernel(scale, x_ref, w_ref, bias_ref, rel_ref, bcol_ref, chosen_ref,
                    probs_ref, mixed_ref, table_ref, ctx_ref, part_ref, sel_ref, far_ref, acc_ref):
    length = x_ref.shape[0]
    cols = ctx_ref.shape[1]
    classes = rel_ref.shape[0]
    span = table_ref.shape[0]
    blocks = length // BLK
    win = length + BLK
    bias = bias_ref[...].astype(F32)
    mixed_ref[...] = (nn(x_ref[...], w_ref[:, : 3 * cols]) + bias).astype(BF16)
    pos = (nn(rel_ref[...], w_ref[:, : 2 * cols]) + bias[:, : 2 * cols]).astype(BF16)
    spread = (bcol_ref[...] == lax.broadcasted_iota(jnp.int32, (span, classes), 1)).astype(BF16)
    table_ref[...] = nn(spread, pos).astype(BF16)
    quarter = chosen_ref.shape[2]
    below = (lax.broadcasted_iota(jnp.int32, (quarter, quarter), 0) <= lax.broadcasted_iota(jnp.int32, (quarter, quarter), 1)).astype(BF16)
    order = lax.broadcasted_iota(jnp.int32, sel_ref.shape[1:], 0).astype(F32) + 1.0
    for q in range(sel_ref.shape[0]):
        rank = nn(chosen_ref[q].astype(BF16), below)[:1]
        sel_ref[q] = jnp.where(rank == order, chosen_ref[q, :1], 0.0).astype(BF16)
    lanes = lax.broadcasted_iota(jnp.int32, (1, cols), 1) // HEAD_DIM
    acc_ref[...] = jnp.zeros_like(acc_ref)

    def head(h, carry):
        own = lanes == h
        pick = lambda v: jnp.where(own, v, jnp.zeros_like(v))
        key_h = pick(mixed_ref[:, cols : 2 * cols])
        for b in range(blocks):
            start = length - BLK * (b + 1)
            rows = slice(BLK * b, BLK * (b + 1))
            wide = nt(key_h[rows], table_ref[start : start + win, :cols])
            turned = pltpu.roll(wide, win - BLK + 1, 1, stride=1, stride_axis=0)[:, :length]
            far_ref[:, rows] = turned.T
        value_h = pick(mixed_ref[:, 2 * cols : 3 * cols])
        for b in range(blocks):
            start = length - BLK * (b + 1)
            rows = slice(BLK * b, BLK * (b + 1))
            query = pick(mixed_ref[rows, :cols])
            wide = nt(query, table_ref[start : start + win, cols : 2 * cols])
            near = pltpu.roll(wide, win - BLK + 1, 1, stride=1, stride_axis=0)[:, :length]
            scores = (nt(query, key_h) + near + far_ref[rows, :]) * scale
            top = jnp.max(scores, -1, keepdims=True)
            weights = jnp.exp(scores - top)
            probs = weights / jnp.sum(weights, -1, keepdims=True)
            probs_ref[h, rows, :] = probs
            acc_ref[rows, :] += nn(probs.astype(BF16), value_h)
        return carry

    lax.fori_loop(0, cols // HEAD_DIM, head, 0)
    ctx_ref[...] = acc_ref[...].astype(BF16)
    part_ref[...] = nt(ctx_ref[...], w_ref[:, 3 * cols :]).astype(BF16)

def attn_fwd(x, w, bias, rel, bcol, chosen, keep):
    length = x.shape[0]
    cols = w.shape[1] // 4
    width = w.shape[0]
    scale = 1.0 / math.sqrt(3 * HEAD_DIM)
    heads = cols // HEAD_DIM
    span = bcol.shape[0]
    S = jax.ShapeDtypeStruct
    return pl.pallas_call(
        functools.partial(attn_fwd_kernel, scale),
        out_shape=(S((heads, length, length), F32), S((length, 3 * cols), BF16), S((span, 2 * cols), BF16),
                   S((length, cols), BF16), S((length, width), BF16), S((chosen.shape[0], keep, chosen.shape[2]), BF16)),
        scratch_shapes=[pltpu.VMEM((length, length), F32), pltpu.VMEM((length, cols), F32)],
        name="attn_fwd",
    )(x, w, bias, rel, bcol, chosen)

def attn_bwd_kernel(scale, x_ref, w_ref, rel_ref, bcol_ref, probs_ref, mixed_ref, table_ref, ctx_ref, rows_ref, sel_ref, past_ref, thr_ref,
                    grads_ref, part_ref, relpart_ref, small_ref,
                    dctx_ref, dctx_t, turn_t, dq_ref, dk_ref, dv_t, dpos_t, ds_ref):
    length = x_ref.shape[0]
    cols = ctx_ref.shape[1]
    classes = rel_ref.shape[0]
    span = table_ref.shape[0]
    blocks = length // BLK
    win = length + BLK
    keep = sel_ref.shape[1]
    flip = (lax.broadcasted_iota(jnp.int32, (BLK, BLK), 0) + lax.broadcasted_iota(jnp.int32, (BLK, BLK), 1) == BLK - 1).astype(BF16)
    small = nn(rows_ref[...], w_ref[:, 3 * cols :]).astype(BF16)
    ctx_small = []
    for b in range(blocks):
        rows = slice(BLK * b, BLK * (b + 1))
        few = slice(keep * b, keep * (b + 1))
        dctx_ref[rows, :] = tn(sel_ref[b], small[few]).astype(BF16)
        ctx_small.append(nn(sel_ref[b], ctx_ref[rows, :]).astype(BF16))
        turn_t[:cols, rows] = tn(mixed_ref[rows, :cols], flip).astype(BF16)
        turn_t[cols:, rows] = tn(mixed_ref[rows, cols : 2 * cols], flip).astype(BF16)
    dctx_t[...] = dctx_ref[...].T
    grads_ref[:, 3 * cols :] = tn(rows_ref[...], jnp.concatenate(ctx_small, 0)).astype(BF16)
    lanes = lax.broadcasted_iota(jnp.int32, (1, cols), 1) // HEAD_DIM
    dq_ref[...] = jnp.zeros_like(dq_ref)
    dk_ref[...] = jnp.zeros_like(dk_ref)
    dpos_t[...] = jnp.zeros_like(dpos_t)
    blank = jnp.zeros((BLK, BLK), F32)

    def head(h, carry):
        own = lanes == h
        pick = lambda v: jnp.where(own, v, jnp.zeros_like(v))
        mine = pl.ds(pl.multiple_of(h * HEAD_DIM, HEAD_DIM), HEAD_DIM)
        key_h = pick(mixed_ref[:, cols : 2 * cols])
        query_h = pick(mixed_ref[:, :cols])
        value = mixed_ref[:, 2 * cols : 3 * cols]
        posq_h = pick(table_ref[:, :cols])
        posk_h = pick(table_ref[:, cols : 2 * cols])
        total = jnp.zeros((HEAD_DIM, length), F32)
        for b in range(blocks):
            start = length - BLK * (b + 1)
            rows = slice(BLK * b, BLK * (b + 1))
            probs = probs_ref[h, rows, :]
            dprobs = nt(pick(dctx_ref[rows, :]), value)
            dscores = (probs * (dprobs - jnp.sum(probs * dprobs, -1, keepdims=True))).astype(BF16)
            ds_ref[rows, :] = dscores
            total += nn(dctx_t[mine, rows], probs.astype(BF16))
            turned = nn(flip, dscores)
            moved = pltpu.roll(jnp.concatenate([turned, blank], 1), 0, 1, stride=1, stride_axis=0).astype(BF16)
            dq_ref[rows, :] += nn(turned.astype(BF16), key_h) + nn(moved, posk_h[start : start + win])
            low = pl.ds(pl.multiple_of(cols + h * HEAD_DIM, HEAD_DIM), HEAD_DIM)
            dpos_t[low, start : start + win] += nn(turn_t[mine, rows], moved)
        dv_t[mine, :] = total
        for b in range(blocks):
            start = length - BLK * (b + 1)
            rows = slice(BLK * b, BLK * (b + 1))
            turned = nt(flip, ds_ref[:, rows])
            moved = pltpu.roll(jnp.concatenate([turned, blank], 1), 0, 1, stride=1, stride_axis=0).astype(BF16)
            dk_ref[rows, :] += nn(turned.astype(BF16), query_h) + nn(moved, posq_h[start : start + win])
            low = pl.ds(pl.multiple_of(cols + h * HEAD_DIM, HEAD_DIM), HEAD_DIM)
            dpos_t[mine, start : start + win] += nn(turn_t[low, rows], moved)
        return carry

    lax.fori_loop(0, cols // HEAD_DIM, head, 0)
    order = lambda ref: jnp.concatenate([nn(flip, (ref[BLK * b : BLK * (b + 1), :] * scale).astype(BF16)).astype(BF16) for b in range(blocks)], 0)
    dmixed = jnp.concatenate([order(dq_ref), order(dk_ref), dv_t[...].T.astype(BF16)], 1)
    spread = (bcol_ref[...] == lax.broadcasted_iota(jnp.int32, (span, classes), 1)).astype(BF16)
    wide = dpos_t[...] * scale
    high = wide.astype(BF16)
    dpos = (nn(high, spread) + nn((wide - high.astype(F32)).astype(BF16), spread)).T
    dpos_low = dpos.astype(BF16)
    sums = jnp.sum(dmixed.astype(F32), 0, keepdims=True)
    small_ref[...] = past_ref[...]
    small_ref[THRESHOLD : THRESHOLD + 1, :] = thr_ref[...]
    small_ref[BIAS : BIAS + 1, : 2 * cols] = sums[:, : 2 * cols] + jnp.sum(dpos, 0, keepdims=True)
    small_ref[BIAS : BIAS + 1, 2 * cols : 3 * cols] = sums[:, 2 * cols :]
    relpart_ref[...] = nt(dpos_low, w_ref[:, : 2 * cols]).astype(BF16)
    part_ref[...] = nt(dmixed, w_ref[:, : 3 * cols]).astype(BF16)
    both = tn(x_ref[...], dmixed)
    grads_ref[:, : 2 * cols] = (both[:, : 2 * cols] + tn(rel_ref[...], dpos_low)).astype(BF16)
    grads_ref[:, 2 * cols : 3 * cols] = both[:, 2 * cols :].astype(BF16)

def attn_bwd(x, w, rel, bcol, probs, mixed, table, ctx, rows, sel, past, thr):
    length, width = x.shape
    cols = w.shape[1] // 4
    scale = 1.0 / math.sqrt(3 * HEAD_DIM)
    span = bcol.shape[0]
    S = jax.ShapeDtypeStruct
    V = pltpu.VMEM
    return pl.pallas_call(
        functools.partial(attn_bwd_kernel, scale),
        out_shape=(S((width, 4 * cols), BF16), S((length, width), BF16), S((rel.shape[0], width), BF16), S(past.shape, F32)),
        scratch_shapes=[V((length, cols), BF16), V((cols, length), BF16), V((2 * cols, length), BF16), V((length, cols), F32), V((length, cols), F32),
                        V((cols, length), F32), V((2 * cols, span), F32), V((length, length), BF16)],
        name="attn_bwd",
    )(x, w, rel, bcol, probs, mixed, table, ctx, rows, sel, past, thr)


MESH = pl.DeviceIdType.MESH


def at_place(spot, n):
    return jnp.where(spot < n // 2, 2 * spot, 2 * (n - 1 - spot) + 1)


def place_of(index, n):
    return jnp.where(index % 2 == 0, index // 2, n - 1 - index // 2)


class Links:
    def __init__(self, n):
        self.n = n
        self.dp = lax.axis_index("dp")
        self.me = lax.axis_index("tensor")
        self.spot = place_of(self.dp, n)
        self.right = (at_place((self.spot + 1) % n, n), self.me)
        self.left = (at_place((self.spot + n - 1) % n, n), self.me)
        self.core = self.me % 2
        self.twin = (self.dp, self.me + 1 - 2 * self.core)
        self.across = (self.dp, (self.me + 2) % 4)

    def chunk(self, shift):
        return at_place((self.spot + shift + 2 * self.n) % self.n, self.n)

    def greet(self, ring, pair):
        peers = ([self.left, self.right] if ring else []) + ([self.twin, self.across] if pair else [])
        barrier = pltpu.get_barrier_semaphore()
        for peer in peers:
            pl.semaphore_signal(barrier, inc=1, device_id=peer, device_id_type=MESH)
        pl.semaphore_wait(barrier, len(peers))


class Sems:
    def __init__(self, send, recv):
        self.send, self.recv, self.used = send, recv, 0

    def copy(self, src, dst, peer):
        k = self.used
        self.used += 1
        return pltpu.make_async_remote_copy(src_ref=src, dst_ref=dst, send_sem=self.send.at[k], recv_sem=self.recv.at[k],
                                            device_id=peer, device_id_type=MESH)


def run_all(*tasks):
    tasks = list(tasks)
    while tasks:
        for task in list(tasks):
            try:
                next(task)
            except StopIteration:
                tasks.remove(task)


def ring_gather(links, sems, full, own=None):
    n = links.n
    half = n // 2
    cut = full.shape[2] // 2
    sides = ((links.right, -1, slice(0, cut)), (links.left, 1, slice(cut, 2 * cut)))
    made = []
    for s in range(half):
        last = s == half - 1
        for k, (peer, step, part) in enumerate(sides):
            if s:
                made[2 * (s - 1) + k].wait_recv()
            index = links.chunk(step * s)
            dst = full.at[index, :, part] if last else full.at[index]
            src = dst if s or own is None else (own.at[:, part] if last else own)
            made.append(sems.copy(src, dst, peer))
            made[-1].start()
        yield
    for k in range(2):
        made[2 * (half - 1) + k].wait_recv()
    for copy in made:
        copy.wait_send()


def ring_scatter(links, sems, parts, slots, done):
    n = links.n
    half = n // 2
    cut = parts.shape[2] // 2
    sides = ((links.right, 1, slice(0, cut), slice(cut, 2 * cut)), (links.left, -1, slice(cut, 2 * cut), slice(0, cut)))
    made = []
    for s in range(half):
        for k, (peer, step, part, rest) in enumerate(sides):
            index = links.chunk(step * (half - s))
            if s == 0:
                src, dst = parts.at[index, :, part], slots.at[k, 0, :, part]
            else:
                made[2 * (s - 1) + k].wait_recv()
                held = slots.at[k, s - 1]
                if s == 1:
                    held[:, part] = (held[:, part].astype(F32) + parts[index, :, part].astype(F32)).astype(BF16)
                    held[:, rest] = parts[index, :, rest]
                else:
                    held[...] = (held[...].astype(F32) + parts[index].astype(F32)).astype(BF16)
                src, dst = held, slots.at[k, s]
            made.append(sems.copy(src, dst, peer))
            made[-1].start()
        yield
    for k in range(2):
        made[2 * (half - 1) + k].wait_recv()
    done(parts[links.dp].astype(F32) + slots[0, half - 1].astype(F32) + slots[1, half - 1].astype(F32))
    for copy in made:
        copy.wait_send()


def group_gather(links, sems, full, own=None):
    mine = full.at[links.me]
    src = mine if own is None else own
    over = sems.copy(src, mine, links.across)
    over.start()
    near = sems.copy(src, mine, links.twin)
    near.start()
    yield
    over.wait_recv()
    block = full.at[(links.me + 2) % 4]
    on = sems.copy(block, block, links.twin)
    on.start()
    yield
    near.wait_recv()
    on.wait_recv()
    for copy in (over, near, on):
        copy.wait_send()


def group_scatter(links, sems, parts, slots, done):
    mine, other = links.me, (links.me + 2) % 4
    twin = links.me + 1 - 2 * links.core
    first = sems.copy(parts.at[(twin + 2) % 4], slots.at[0], links.twin)
    first.start()
    second = sems.copy(parts.at[twin], slots.at[1], links.twin)
    second.start()
    yield
    first.wait_recv()
    slots[0] = (slots[0].astype(F32) + parts[other].astype(F32)).astype(BF16)
    over = sems.copy(slots.at[0], slots.at[2], links.across)
    over.start()
    yield
    second.wait_recv()
    over.wait_recv()
    done(parts[mine].astype(F32) + slots[1].astype(F32) + slots[2].astype(F32))
    for copy in (first, second, over):
        copy.wait_send()


def comm_call(kernel, ident, outs, scratch, sems, args, name):
    return pl.pallas_call(
        kernel,
        out_shape=outs,
        scratch_shapes=list(scratch) + [pltpu.SemaphoreType.DMA((sems,)), pltpu.SemaphoreType.DMA((sems,))],
        compiler_params=pltpu.CompilerParams(collective_id=ident, has_side_effects=True),
        name=name,
    )(*args)


def normalize(value, gain, shift):
    mean = jnp.mean(value, -1, keepdims=True)
    center = value - mean
    inverse = lax.rsqrt(jnp.mean(center * center, -1, keepdims=True) + EPSILON)
    unit = center * inverse
    return (unit * gain + shift, unit, inverse)


def normalize_back(incoming, gain, unit, inverse):
    scaled = incoming * gain
    result = inverse * (scaled - jnp.mean(scaled, -1, keepdims=True) - unit * jnp.mean(scaled * unit, -1, keepdims=True))
    return (result, jnp.sum(incoming * unit, 0, keepdims=True), jnp.sum(incoming, 0, keepdims=True))


OFFSET, RESIDUE, STRETCH, UPLIFT, AMPLIFY, DISPLACE, THRESHOLD, BIAS = range(8)


def row(ref, k):
    return ref[k : k + 1, :]


def enter_kernel(n, tok_ref, own_ref, pick_ref, x_ref, w_ref, chosen_ref, send, recv):
    links, sems = Links(n), Sems(send, recv)
    links.greet(True, True)
    x_ref[links.me] = tok_ref[...]
    w_ref[links.dp] = own_ref[...]
    chosen_ref[links.me] = pick_ref[...]
    run_all(group_gather(links, sems, x_ref, tok_ref), ring_gather(links, sems, w_ref, own_ref), group_gather(links, sems, chosen_ref, pick_ref))


def mid_kernel(n, part_ref, tok_ref, par_ref, hidden_ref, mid_ref, unit_ref, inverse_ref, slots, send, recv):
    links, sems = Links(n), Sems(send, recv)
    links.greet(False, True)

    def done(total):
        mid, unit, inverse = normalize(tok_ref[...].astype(F32) + total + row(par_ref, OFFSET), row(par_ref, STRETCH), row(par_ref, UPLIFT))
        mid_ref[...] = mid
        unit_ref[...] = unit
        inverse_ref[...] = jnp.broadcast_to(inverse, inverse_ref.shape)
        hidden_ref[links.me] = mid.astype(BF16)

    run_all(group_scatter(links, sems, part_ref, slots, done))
    run_all(group_gather(links, sems, hidden_ref))


def end_kernel(n, part_ref, mid_ref, cot_ref, sel_ref, par_ref, result_ref, dend_ref, rows_ref, small_ref, slots, send, recv):
    links, sems = Links(n), Sems(send, recv)
    links.greet(False, True)
    mine = sel_ref[links.me]
    marks = tn(mine, jnp.ones((mine.shape[0], 128), BF16))[:, :1]

    def done(total):
        value, unit, inverse = normalize(mid_ref[...] + total + row(par_ref, RESIDUE), row(par_ref, AMPLIFY), row(par_ref, DISPLACE))
        result_ref[...] = value.astype(BF16)
        upstream = cot_ref[...].astype(F32) * marks
        d_end, gain, shift = normalize_back(upstream, row(par_ref, AMPLIFY), unit, inverse)
        dend_ref[...] = d_end
        low = d_end.astype(BF16)
        rows_ref[links.me] = nn(mine, low).astype(BF16)
        small_ref[...] = jnp.zeros_like(small_ref)
        small_ref[AMPLIFY : AMPLIFY + 1, :] = gain
        small_ref[DISPLACE : DISPLACE + 1, :] = shift
        small_ref[RESIDUE : RESIDUE + 1, :] = jnp.sum(low.astype(F32), 0, keepdims=True)

    run_all(group_scatter(links, sems, part_ref, slots, done))
    run_all(group_gather(links, sems, rows_ref))


def back_kernel(n, part_ref, dend_ref, unit_ref, inverse_ref, sel_ref, par_ref, past_ref, dmid_ref, rows_ref, small_ref, slots, send, recv):
    links, sems = Links(n), Sems(send, recv)
    links.greet(False, True)
    mine = sel_ref[links.me]

    def done(total):
        high = total.astype(BF16)
        spread = tn(mine, high) + tn(mine, (total - high.astype(F32)).astype(BF16))
        d_mid, gain, shift = normalize_back(dend_ref[...] + spread, row(par_ref, STRETCH), unit_ref[...], inverse_ref[:, :1])
        dmid_ref[...] = d_mid
        low = d_mid.astype(BF16)
        rows_ref[links.me] = nn(mine, low).astype(BF16)
        small_ref[...] = past_ref[...]
        small_ref[STRETCH : STRETCH + 1, :] = gain
        small_ref[UPLIFT : UPLIFT + 1, :] = shift
        small_ref[OFFSET : OFFSET + 1, :] = jnp.sum(low.astype(F32), 0, keepdims=True)

    run_all(group_scatter(links, sems, part_ref, slots, done))
    run_all(group_gather(links, sems, rows_ref))


def total_kernel(n, dexp_ref, dred_ref, exp_ref, red_ref, exp_slots, red_slots, send, recv):
    links, sems = Links(n), Sems(send, recv)
    links.greet(True, False)

    def total(parts, slots, full):
        def done(value):
            full[links.dp] = value.astype(BF16)

        yield from ring_scatter(links, sems, parts, slots, done)
        yield from ring_gather(links, sems, full)

    run_all(total(dexp_ref, exp_slots, exp_ref), total(dred_ref, red_slots, red_ref))


def exit_kernel(n, grads_ref, tok_ref, rel_ref, small_ref, dmid_ref, weights_ref, tokens_ref, relative_ref, sums_ref,
                grad_slots, tok_slots, rel_slots, rel_own, rel_ring, small_all, small_slots, send, recv):
    links, sems = Links(n), Sems(send, recv)
    links.greet(True, True)

    def grads_done(total):
        weights_ref[...] = total

    def tokens_done(total):
        tokens_ref[...] = dmid_ref[...] + total

    def rel_done(total):
        rel_own[...] = total.astype(BF16).reshape(rel_own.shape)

    def small():
        shared = lax.broadcasted_iota(jnp.int32, small_ref.shape, 0) < THRESHOLD
        a = sems.copy(small_ref, small_slots.at[0], links.twin)
        a.start()
        yield
        a.wait_recv()
        small_slots[1] = small_ref[...] + jnp.where(shared, small_slots[0], 0.0)
        b = sems.copy(small_slots.at[1], small_slots.at[2], links.across)
        b.start()
        yield
        b.wait_recv()
        small_all[links.dp] = small_slots[1] + jnp.where(shared, small_slots[2], 0.0)
        yield from ring_gather(links, sems, small_all)
        a.wait_send()
        b.wait_send()
        sums_ref[...] = jnp.sum(small_all[...], 0)

    def relative():
        yield from group_scatter(links, sems, rel_ref, rel_slots, rel_done)

        def own_done(total):
            place = relative_ref.at[links.me]
            place[links.dp] = total.astype(BF16)

        yield from ring_scatter(links, sems, rel_own, rel_ring, own_done)
        yield from ring_gather(links, sems, relative_ref.at[links.me])
        yield from group_gather(links, sems, relative_ref)

    run_all(relative(), small(), ring_scatter(links, sems, grads_ref, grad_slots, grads_done), group_scatter(links, sems, tok_ref, tok_slots, tokens_done))


def cumulative(inner):
    return 0.5 * (1.0 + lax.erf(inner * (1.0 / math.sqrt(2.0))))


def ff_fwd_kernel(hidden_ref, exp_ref, red_ref, par_ref, feed_ref):
    rows = hidden_ref.shape[0] // 2
    bent = row(par_ref, THRESHOLD)

    def block(b, carry):
        here = pl.ds(pl.multiple_of(b * rows, rows), rows)
        inner = nn(hidden_ref[here, :], exp_ref[...]) + bent
        feed_ref[here, :] = nn((inner * cumulative(inner)).astype(BF16), red_ref[...]).astype(BF16)
        return carry

    lax.fori_loop(0, 2, block, 0)


def ff_bwd_kernel(hidden_ref, rows_ref, sel_ref, exp_ref, red_ref, par_ref, back_ref, dexp_ref, dred_ref, thr_ref):
    groups = sel_ref.shape[0]
    few = jnp.concatenate([nn(sel_ref[q], hidden_ref[q]).astype(BF16) for q in range(groups)], 0)
    inner = nn(few, exp_ref[...]) + row(par_ref, THRESHOLD)
    weight = cumulative(inner)
    active = (inner * weight).astype(BF16)
    slope = weight + inner * jnp.exp(-0.5 * inner * inner) * (1.0 / math.sqrt(2.0 * math.pi))
    rows = rows_ref[...]
    d_inner = (nt(rows, red_ref[...]) * slope).astype(BF16)
    back_ref[...] = nt(d_inner, exp_ref[...]).astype(BF16)
    thr_ref[...] = jnp.sum(d_inner.astype(F32), 0, keepdims=True)
    dexp_ref[...] = tn(few, d_inner).astype(BF16)
    dred_ref[...] = tn(active, rows).astype(BF16)


def shards(tokens, cotangent, selected, buckets, projector, intercepts, combiner, offset, relative, stretch, uplift,
           expander, threshold, reducer, residue, amplify, displace):
    quarter, width = tokens.shape
    cols = projector.shape[2]
    part = projector.shape[1]
    n, group = lax.axis_size("dp"), lax.axis_size("tensor")
    classes = relative.shape[0]
    keep = -(-(quarter * 2 // 5) // 16) * 16
    S, V = jax.ShapeDtypeStruct, pltpu.VMEM
    packed = jnp.concatenate([projector[0], projector[1], projector[2], combiner], 1)
    picks = jnp.broadcast_to(selected.astype(F32)[None, :], (8, quarter))
    bias = intercepts.reshape(1, 3 * cols)
    span = buckets.shape[0] + 1
    bcol = jnp.concatenate([buckets[::-1], jnp.full((1,), -1, jnp.int32)]).reshape(span, 1)
    params = jnp.stack([v.astype(F32) for v in (offset, residue, stretch, uplift, amplify, displace, threshold, threshold)])

    x, w, chosen = comm_call(
        functools.partial(enter_kernel, n), 1,
        (S((group, quarter, width), BF16), S((n, part, width), BF16), S((group, 8, quarter), F32)),
        [], n + 8, (tokens, packed, picks), "enter")
    x2, w2 = x.reshape(group * quarter, width), w.reshape(n * part, width)
    probs, mixed, table, ctx, first, sel = attn_fwd(x2, w2, bias, relative, bcol, chosen, keep)
    hidden, mid, unit, inverse = comm_call(
        functools.partial(mid_kernel, n), 2,
        (S((group, quarter, width), BF16), S((quarter, width), F32), S((quarter, width), F32), S((quarter, 128), F32)),
        [V((3, quarter, width), BF16)], 8, (first.reshape(group, quarter, width), tokens, params), "mid")
    feed = pl.pallas_call(ff_fwd_kernel, out_shape=S((group * quarter, width), BF16), name="ff_fwd")(
        hidden.reshape(group * quarter, width), expander, reducer, params)
    result, d_end, d_rows, small = comm_call(
        functools.partial(end_kernel, n), 3,
        (S((quarter, width), BF16), S((quarter, width), F32), S((group, keep, width), BF16), S((8, width), F32)),
        [V((3, quarter, width), BF16)], 8, (feed.reshape(group, quarter, width), mid, cotangent, sel, params), "end")
    back, dexp, dred, thr = pl.pallas_call(
        ff_bwd_kernel,
        out_shape=(S((group * keep, width), BF16), S(expander.shape, BF16), S(reducer.shape, BF16), S((1, threshold.shape[0]), F32)),
        name="ff_bwd")(hidden, d_rows.reshape(group * keep, width), sel, expander, reducer, params)
    d_mid, d_attn, small = comm_call(
        functools.partial(back_kernel, n), 4,
        (S((quarter, width), F32), S((group, keep, width), BF16), S((8, width), F32)),
        [V((3, keep, width), BF16)], 8, (back.reshape(group, keep, width), d_end, unit, inverse, sel, params, small), "back")
    grads, input_part, rel_part, small = attn_bwd(x2, w2, relative, bcol, probs, mixed, table, ctx, d_attn.reshape(group * keep, width), sel, small, thr)
    ring = (n, width // n, width)
    totals = comm_call(
        functools.partial(total_kernel, n), 5,
        (S((n, expander.shape[0] // n, width), BF16), S((n, reducer.shape[0] // n, width), BF16)),
        [V((2, n // 2, expander.shape[0] // n, width), BF16), V((2, n // 2, reducer.shape[0] // n, width), BF16)],
        4 * n, (dexp.reshape(n, -1, width), dred.reshape(n, -1, width)), "totals")
    lines = classes // group // n
    weights, tokens_grad, relative_grad, sums = comm_call(
        functools.partial(exit_kernel, n), 6,
        (S((part, width), F32), S((quarter, width), F32), S((group, n, lines, width), BF16), S((8, width), F32)),
        [V((2, n // 2, part, width), BF16), V((3, quarter, width), BF16), V((3, classes // group, width), BF16), V((n, lines, width), BF16),
         V((2, n // 2, lines, width), BF16), V((n, 8, width), F32), V((3, 8, width), F32)],
        4 * n + 16, (grads.reshape(n, part, width), input_part.reshape(group, quarter, width), rel_part.reshape(group, classes // group, width), small, d_mid), "exit")
    projector_grad = jnp.stack([weights[:, :cols], weights[:, cols : 2 * cols], weights[:, 2 * cols : 3 * cols]])
    return (result, tokens_grad, projector_grad, sums[BIAS, : 3 * cols].reshape(3, cols), weights[:, 3 * cols :], sums[OFFSET],
            relative_grad.astype(F32).reshape(classes, width), sums[STRETCH], sums[UPLIFT], totals[0].astype(F32).reshape(expander.shape),
            sums[THRESHOLD], totals[1].astype(F32).reshape(reducer.shape), sums[RESIDUE], sums[AMPLIFY], sums[DISPLACE])


def solution(mesh):
    both = P(("dp", "tensor"), None)
    return jax.shard_map(
        shards,
        mesh=mesh,
        in_specs=(both, both, P(("dp", "tensor")), P(), P(None, "dp", "tensor"), P(None, "tensor"), P("dp", "tensor"), P(), P(), P(), P(),
                  P(None, "tensor"), P("tensor"), P("tensor", None), P(), P(), P()),
        out_specs=(both, both, P(None, "dp", "tensor"), P(None, "tensor"), P("dp", "tensor"), P(), P(), P(), P(),
                   P(None, "tensor"), P("tensor"), P("tensor", None), P(), P(), P()),
        check_vma=False,
    )
```

```python
import functools
import math
from types import SimpleNamespace

import jax
import jax.numpy as jnp
from jax import lax
from jax.experimental import pallas as pl
from jax.experimental.pallas import tpu as pltpu
from jax.sharding import PartitionSpec as P

HEAD_DIM = 64
BLK = 128
EPSILON = 1e-05
F32, BF16 = jnp.float32, jnp.bfloat16
MESH = pl.DeviceIdType.MESH
OFFSET, RESIDUE, STRETCH, UPLIFT, AMPLIFY, DISPLACE, THRESHOLD, BIAS = range(8)


def nn(a, b):
    return lax.dot_general(a, b, (((1,), (0,)), ((), ())), preferred_element_type=F32)


def nt(a, b):
    return lax.dot_general(a, b, (((1,), (1,)), ((), ())), preferred_element_type=F32)


def tn(a, b):
    return lax.dot_general(a, b, (((0,), (0,)), ((), ())), preferred_element_type=F32)


def flat(value):
    return value.reshape(value.shape[0] * value.shape[1], value.shape[2])


def line(ref):
    return ref[...].astype(F32).reshape(1, -1)


def exchange():
    return (lax.broadcasted_iota(jnp.int32, (BLK, BLK), 0) + lax.broadcasted_iota(jnp.int32, (BLK, BLK), 1) == BLK - 1).astype(BF16)


def at_place(spot, n):
    return jnp.where(spot < n // 2, 2 * spot, 2 * (n - 1 - spot) + 1)


def place_of(index, n):
    return jnp.where(index % 2 == 0, index // 2, n - 1 - index // 2)


class Links:
    def __init__(self, n, send, recv):
        self.n, self.send, self.recv, self.used = n, send, recv, 0
        self.dp = lax.axis_index("dp")
        self.me = lax.axis_index("tensor")
        self.spot = place_of(self.dp, n)
        self.right = (at_place((self.spot + 1) % n, n), self.me)
        self.left = (at_place((self.spot + n - 1) % n, n), self.me)
        core = self.me % 2
        self.mate = self.me + 1 - 2 * core
        self.other = (self.me + 2) % 4
        self.twin = (self.dp, self.mate)
        self.across = (self.dp, self.other)

    def chunk(self, shift):
        return at_place((self.spot + shift + 2 * self.n) % self.n, self.n)

    def greet(self):
        barrier = pltpu.get_barrier_semaphore()
        for peer in (self.left, self.right, self.twin, self.across):
            pl.semaphore_signal(barrier, inc=1, device_id=peer, device_id_type=MESH)
        pl.semaphore_wait(barrier, 4)

    def start(self, src, dst, peer):
        k = self.used
        self.used += 1
        copy = pltpu.make_async_remote_copy(src_ref=src, dst_ref=dst, send_sem=self.send.at[k], recv_sem=self.recv.at[k],
                                            device_id=peer, device_id_type=MESH)
        copy.start()
        return copy


def step(*tasks):
    for task in tasks:
        next(task, None)


def finish(*tasks):
    tasks = list(tasks)
    while tasks:
        for task in list(tasks):
            try:
                next(task)
            except StopIteration:
                tasks.remove(task)


def ring_gather(links, full, low, high, cut, own=None):
    n = links.n
    half = n // 2
    sides = ((links.right, -1, slice(low, cut)), (links.left, 1, slice(cut, high)))
    made = []
    for s in range(half):
        for k, (peer, way, part) in enumerate(sides):
            if s:
                made[2 * (s - 1) + k].wait_recv()
            index = links.chunk(way * s)
            if s < half - 1:
                part = slice(low, high)
            dst = full.at[index, :, part]
            made.append(links.start(dst if s or own is None else own.at[:, part], dst, peer))
        yield
    for k in range(2):
        made[2 * (half - 1) + k].wait_recv()
    for copy in made:
        copy.wait_send()


def ring_scatter(links, parts, slots, done, low, high, cut):
    n = links.n
    half = n // 2
    sides = ((links.right, 1, slice(low, cut), slice(cut, high)), (links.left, -1, slice(cut, high), slice(low, cut)))
    here = slice(low, high)
    made = []
    for s in range(half):
        for k, (peer, way, part, rest) in enumerate(sides):
            index = links.chunk(way * (half - s))
            if s == 0:
                src, dst = parts.at[index, :, part], slots.at[k, 0, :, part]
            else:
                made[2 * (s - 1) + k].wait_recv()
                held = slots.at[k, s - 1]
                if s == 1:
                    held[:, part] = (held[:, part].astype(F32) + parts[index, :, part].astype(F32)).astype(BF16)
                    held[:, rest] = parts[index, :, rest]
                else:
                    held[:, here] = (held[:, here].astype(F32) + parts[index, :, here].astype(F32)).astype(BF16)
                src, dst = held.at[:, here], slots.at[k, s, :, here]
            made.append(links.start(src, dst, peer))
        yield
    for k in range(2):
        made[2 * (half - 1) + k].wait_recv()
    done(parts[links.dp, :, here].astype(F32) + slots[0, half - 1, :, here].astype(F32) + slots[1, half - 1, :, here].astype(F32))
    for copy in made:
        copy.wait_send()


def group_gather(links, full, own=None):
    mine = full.at[links.me]
    src = mine if own is None else own
    over = links.start(src, mine, links.across)
    near = links.start(src, mine, links.twin)
    yield
    over.wait_recv()
    block = full.at[links.other]
    on = links.start(block, block, links.twin)
    yield
    near.wait_recv()
    on.wait_recv()
    for copy in (over, near, on):
        copy.wait_send()


def group_scatter(links, parts, slots, done):
    first = links.start(parts.at[(links.mate + 2) % 4], slots.at[0], links.twin)
    second = links.start(parts.at[links.mate], slots.at[1], links.twin)
    yield
    first.wait_recv()
    slots[0] = (slots[0].astype(F32) + parts[links.other].astype(F32)).astype(BF16)
    over = links.start(slots.at[0], slots.at[2], links.across)
    yield
    second.wait_recv()
    over.wait_recv()
    done(parts[links.me].astype(F32) + slots[1].astype(F32) + slots[2].astype(F32))
    for copy in (first, second, over):
        copy.wait_send()


def normalize(value, gain, shift):
    mean = jnp.mean(value, -1, keepdims=True)
    center = value - mean
    inverse = lax.rsqrt(jnp.mean(center * center, -1, keepdims=True) + EPSILON)
    unit = center * inverse
    return (unit * gain + shift, unit, inverse)


def normalize_back(incoming, gain, unit, inverse):
    scaled = incoming * gain
    result = inverse * (scaled - jnp.mean(scaled, -1, keepdims=True) - unit * jnp.mean(scaled * unit, -1, keepdims=True))
    return (result, jnp.sum(incoming * unit, 0, keepdims=True), jnp.sum(incoming, 0, keepdims=True))


def cumulative(inner):
    return 0.5 * (1.0 + lax.erf(inner * (1.0 / math.sqrt(2.0))))


def enter(links, c):
    cols = c.combiner.shape[1]
    for m in range(3):
        c.own[:, cols * m : cols * (m + 1)] = c.projector[m]
    c.own[:, 3 * cols :] = c.combiner[...]
    c.pick[...] = jnp.broadcast_to(c.selected[...].astype(F32).reshape(1, -1), c.pick.shape)
    links.greet()
    c.x[links.me] = c.tokens[...]
    c.w[links.dp] = c.own[...]
    c.chosen[links.me] = c.pick[...]
    width = c.own.shape[1]
    finish(group_gather(links, c.x, c.tokens), ring_gather(links, c.w, 0, width // 2, width // 2 - BLK, c.own),
           ring_gather(links, c.w, width // 2, width, width // 2 + BLK, c.own), group_gather(links, c.chosen, c.pick))


def attend(links, c, scale):
    length = c.mixed.shape[0]
    cols = c.combiner.shape[1]
    classes = c.relative.shape[0]
    blocks = length // BLK
    win = length + BLK
    flip = exchange()
    bias = jnp.concatenate([c.intercepts[m : m + 1, :].astype(F32) for m in range(3)], 1)
    weights = flat(c.w[...])
    c.mixed[...] = (nn(flat(c.x[...]), weights[:, : 3 * cols]) + bias).astype(BF16)
    pos = (nn(c.relative[...], weights[:, : 2 * cols]) + bias[:, : 2 * cols]).astype(BF16)
    turned = c.buckets[...].astype(F32).T
    groups = c.buckets.shape[0]
    kinds = lax.broadcasted_iota(jnp.int32, (BLK, classes), 1).astype(F32)
    for g in range(groups):
        rows = slice(BLK * (groups - 1 - g), BLK * (groups - g))
        c.spread[rows, :] = nn(flip, (turned[:, g : g + 1] == kinds).astype(BF16)).astype(BF16)
        c.table[rows, :] = nn(c.spread[rows, :], pos).astype(BF16)
    quarter = c.chosen.shape[2]
    below = (lax.broadcasted_iota(jnp.int32, (quarter, quarter), 0) <= lax.broadcasted_iota(jnp.int32, (quarter, quarter), 1)).astype(BF16)
    order = lax.broadcasted_iota(jnp.int32, c.sel.shape[1:], 0).astype(F32) + 1.0
    for q in range(c.sel.shape[0]):
        rank = nn(c.chosen[q].astype(BF16), below)[:1]
        c.sel[q] = jnp.where(rank == order, c.chosen[q, :1], 0.0).astype(BF16)
    lanes = lax.broadcasted_iota(jnp.int32, (1, cols), 1) // HEAD_DIM
    c.acc[...] = jnp.zeros_like(c.acc)

    def head(h):
        own = lanes == h
        pick = lambda v: jnp.where(own, v, jnp.zeros_like(v))
        key_h = pick(c.mixed[:, cols : 2 * cols])
        for b in range(blocks):
            start = length - BLK * (b + 1)
            rows = slice(BLK * b, BLK * (b + 1))
            wide = nt(key_h[rows], c.table[start : start + win, :cols])
            c.far[:, rows] = pltpu.roll(wide, win - BLK + 1, 1, stride=1, stride_axis=0)[:, :length].T
        value_h = pick(c.mixed[:, 2 * cols : 3 * cols])
        for b in range(blocks):
            start = length - BLK * (b + 1)
            rows = slice(BLK * b, BLK * (b + 1))
            query = pick(c.mixed[rows, :cols])
            wide = nt(query, c.table[start : start + win, cols : 2 * cols])
            near = pltpu.roll(wide, win - BLK + 1, 1, stride=1, stride_axis=0)[:, :length]
            scores = (nt(query, key_h) + near + c.far[rows, :]) * scale
            top = jnp.max(scores, -1, keepdims=True)
            weights = jnp.exp(scores - top)
            probs = weights / jnp.sum(weights, -1, keepdims=True)
            c.probs[h, rows, :] = probs
            c.acc[rows, :] += nn(probs.astype(BF16), value_h)

    for h in range(cols // HEAD_DIM):
        head(h)
    c.ctx[...] = c.acc[...].astype(BF16)
    c.part[...] = nt(c.ctx[...], weights[:, 3 * cols :]).astype(BF16).reshape(c.part.shape)


def middle(links, c):
    def done(total):
        mid, unit, inverse = normalize(c.tokens[...].astype(F32) + total + line(c.offset), line(c.stretch), line(c.uplift))
        c.mid[...] = mid
        c.unit[...] = unit
        c.inverse[...] = jnp.broadcast_to(inverse, c.inverse.shape)
        c.hidden[links.me] = mid.astype(BF16)

    finish(group_scatter(links, c.part, c.part_slots, done))
    finish(group_gather(links, c.hidden))


def feed(links, c):
    bent = line(c.threshold)
    for b in range(2):
        inner = nn(flat(c.hidden[2 * b : 2 * b + 2]), c.expander[...]) + bent
        value = nn((inner * cumulative(inner)).astype(BF16), c.reducer[...]).astype(BF16)
        c.feed[2 * b : 2 * b + 2] = value.reshape((2,) + c.feed.shape[1:])


def end(links, c):
    mine = c.sel[links.me]
    marks = tn(mine, jnp.ones((mine.shape[0], BLK), BF16))[:, :1]

    def done(total):
        value, unit, inverse = normalize(c.mid[...] + total + line(c.residue), line(c.amplify), line(c.displace))
        c.result[...] = value.astype(BF16)
        d_end, gain, shift = normalize_back(c.cotangent[...].astype(F32) * marks, line(c.amplify), unit, inverse)
        c.d_end[...] = d_end
        low = d_end.astype(BF16)
        c.d_rows[links.me] = nn(mine, low).astype(BF16)
        c.small[AMPLIFY : AMPLIFY + 1, :] = gain
        c.small[DISPLACE : DISPLACE + 1, :] = shift
        c.small[RESIDUE : RESIDUE + 1, :] = jnp.sum(low.astype(F32), 0, keepdims=True)

    finish(group_scatter(links, c.feed, c.feed_slots, done))
    finish(group_gather(links, c.d_rows))


def feed_back(links, c):
    few = jnp.concatenate([nn(c.sel[q], c.hidden[q]).astype(BF16) for q in range(c.sel.shape[0])], 0)
    inner = nn(few, c.expander[...]) + line(c.threshold)
    weight = cumulative(inner)
    active = (inner * weight).astype(BF16)
    slope = weight + inner * jnp.exp(-0.5 * inner * inner) * (1.0 / math.sqrt(2.0 * math.pi))
    rows = flat(c.d_rows[...])
    d_inner = (nt(rows, c.reducer[...]) * slope).astype(BF16)
    c.back[...] = nt(d_inner, c.expander[...]).astype(BF16).reshape(c.back.shape)
    c.small[THRESHOLD : THRESHOLD + 1, :] = jnp.sum(d_inner.astype(F32), 0, keepdims=True)
    c.d_exp[...] = tn(few, d_inner).astype(BF16).reshape(c.d_exp.shape)
    c.d_red[...] = tn(active, rows).astype(BF16).reshape(c.d_red.shape)


def total(links, parts, slots, full, cut):
    def done(value):
        full[links.dp] = value.astype(BF16)

    width = parts.shape[2]
    yield from ring_scatter(links, parts, slots, done, 0, width, cut)
    yield from ring_gather(links, full, 0, width, cut)


def middle_back(links, c, beside):
    mine = c.sel[links.me]

    def done(total):
        high = total.astype(BF16)
        spread = tn(mine, high) + tn(mine, (total - high.astype(F32)).astype(BF16))
        d_mid, gain, shift = normalize_back(c.d_end[...] + spread, line(c.stretch), c.unit[...], c.inverse[:, :1])
        c.d_mid[...] = d_mid
        low = d_mid.astype(BF16)
        c.d_attn[links.me] = nn(mine, low).astype(BF16)
        c.small[STRETCH : STRETCH + 1, :] = gain
        c.small[UPLIFT : UPLIFT + 1, :] = shift
        c.small[OFFSET : OFFSET + 1, :] = jnp.sum(low.astype(F32), 0, keepdims=True)

    task = group_scatter(links, c.back, c.back_slots, done)
    step(task)
    step(*beside)
    finish(task)
    task = group_gather(links, c.d_attn)
    step(task)
    step(*beside)
    finish(task)


def attend_back(links, c, scale, beside, leave):
    length = c.mixed.shape[0]
    cols = c.combiner.shape[1]
    span = c.table.shape[0]
    blocks = length // BLK
    win = length + BLK
    flip = exchange()
    weights = flat(c.w[...])
    d_attn = flat(c.d_attn[...])
    little = nn(d_attn, weights[:, 3 * cols :]).astype(BF16)
    keep = c.sel.shape[1]
    ctx_few = []
    for b in range(blocks):
        rows = slice(BLK * b, BLK * (b + 1))
        c.dctx[rows, :] = tn(c.sel[b], little[keep * b : keep * (b + 1)]).astype(BF16)
        ctx_few.append(nn(c.sel[b], c.ctx[rows, :]).astype(BF16))
        c.turn_t[:cols, rows] = tn(c.mixed[rows, :cols], flip).astype(BF16)
        c.turn_t[cols:, rows] = tn(c.mixed[rows, cols : 2 * cols], flip).astype(BF16)
    c.dctx_t[...] = c.dctx[...].T
    lanes = lax.broadcasted_iota(jnp.int32, (1, cols), 1) // HEAD_DIM
    c.dq[...] = jnp.zeros_like(c.dq)
    c.dk[...] = jnp.zeros_like(c.dk)
    c.dpos_t[...] = jnp.zeros_like(c.dpos_t)
    blank = jnp.zeros((BLK, BLK), F32)

    def head(h):
        own = lanes == h
        pick = lambda v: jnp.where(own, v, jnp.zeros_like(v))
        mine = slice(h * HEAD_DIM, (h + 1) * HEAD_DIM)
        low = slice(cols + h * HEAD_DIM, cols + (h + 1) * HEAD_DIM)
        key_h = pick(c.mixed[:, cols : 2 * cols])
        query_h = pick(c.mixed[:, :cols])
        value = c.mixed[:, 2 * cols : 3 * cols]
        posq_h = pick(c.table[:, :cols])
        posk_h = pick(c.table[:, cols : 2 * cols])
        so_far = jnp.zeros((HEAD_DIM, length), F32)
        for b in range(blocks):
            start = length - BLK * (b + 1)
            rows = slice(BLK * b, BLK * (b + 1))
            probs = c.probs[h, rows, :]
            dprobs = nt(pick(c.dctx[rows, :]), value)
            dscores = (probs * (dprobs - jnp.sum(probs * dprobs, -1, keepdims=True))).astype(BF16)
            c.ds[rows, :] = dscores
            so_far += nn(c.dctx_t[mine, rows], probs.astype(BF16))
            turned = nn(flip, dscores)
            moved = pltpu.roll(jnp.concatenate([turned, blank], 1), 0, 1, stride=1, stride_axis=0).astype(BF16)
            c.dq[rows, :] += nn(turned.astype(BF16), key_h) + nn(moved, posk_h[start : start + win])
            c.dpos_t[low, start : start + win] += nn(c.turn_t[mine, rows], moved)
        c.dv_t[mine, :] = so_far
        for b in range(blocks):
            start = length - BLK * (b + 1)
            rows = slice(BLK * b, BLK * (b + 1))
            turned = nt(flip, c.ds[:, rows])
            moved = pltpu.roll(jnp.concatenate([turned, blank], 1), 0, 1, stride=1, stride_axis=0).astype(BF16)
            c.dk[rows, :] += nn(turned.astype(BF16), query_h) + nn(moved, posq_h[start : start + win])
            c.dpos_t[mine, start : start + win] += nn(c.turn_t[low, rows], moved)

    for h in range(cols // HEAD_DIM):
        step(*beside)
        head(h)
    wide = c.dpos_t[...] * scale
    high = wide.astype(BF16)
    dpos = (nn(high, c.spread[...]) + nn((wide - high.astype(F32)).astype(BF16), c.spread[...])).T
    dpos_low = dpos.astype(BF16)
    c.rel_part[...] = nt(dpos_low, weights[:, : 2 * cols]).astype(BF16).reshape(c.rel_part.shape)
    leave("relative")
    order = lambda ref: jnp.concatenate([nn(flip, (ref[BLK * b : BLK * (b + 1), :] * scale).astype(BF16)).astype(BF16) for b in range(blocks)], 0)
    dmixed = jnp.concatenate([order(c.dq), order(c.dk), c.dv_t[...].T.astype(BF16)], 1)
    both = tn(flat(c.x[...]), dmixed)
    grads = jnp.concatenate([both[:, : 2 * cols] + tn(c.relative[...], dpos_low), both[:, 2 * cols :], tn(d_attn, jnp.concatenate(ctx_few, 0))], 1)
    c.grads[...] = grads.astype(BF16).reshape(c.grads.shape)
    leave("grads")
    c.in_part[...] = nt(dmixed, weights[:, : 3 * cols]).astype(BF16).reshape(c.in_part.shape)
    leave("tokens")
    sums = jnp.sum(dmixed.astype(F32), 0, keepdims=True)
    c.small[BIAS : BIAS + 1, : 2 * cols] = sums[:, : 2 * cols] + jnp.sum(dpos, 0, keepdims=True)
    c.small[BIAS : BIAS + 1, 2 * cols : 3 * cols] = sums[:, 2 * cols :]
    c.small[BIAS : BIAS + 1, 3 * cols :] = jnp.zeros((1, cols), F32)
    leave("small")


def leave_small(links, c):
    shared = lax.broadcasted_iota(jnp.int32, c.small.shape, 0) < THRESHOLD
    a = links.start(c.small, c.small_slots.at[0], links.twin)
    yield
    a.wait_recv()
    c.small_slots[1] = c.small[...] + jnp.where(shared, c.small_slots[0], 0.0)
    b = links.start(c.small_slots.at[1], c.small_slots.at[2], links.across)
    yield
    b.wait_recv()
    c.small_all[links.dp] = c.small_slots[1] + jnp.where(shared, c.small_slots[2], 0.0)
    yield from ring_gather(links, c.small_all, 0, c.small.shape[1], c.small.shape[1] // 2)
    a.wait_send()
    b.wait_send()
    c.sums[...] = jnp.sum(c.small_all[...], 0)


def leave_relative(links, c):
    def rel_done(total):
        c.rel_own[...] = total.astype(BF16).reshape(c.rel_own.shape)

    yield from group_scatter(links, c.rel_part, c.rel_slots, rel_done)
    mine = c.rel_all.at[links.me]

    def own_done(total):
        mine[links.dp] = total.astype(BF16)

    width = c.rel_own.shape[2]
    yield from ring_scatter(links, c.rel_own, c.rel_ring, own_done, 0, width, width // 2)
    yield from ring_gather(links, mine, 0, width, width // 2)
    yield from group_gather(links, c.rel_all)


def layer_kernel(n, names, *refs):
    c = SimpleNamespace(**dict(zip(names, refs)))
    links = Links(n, c.send, c.recv)
    scale = 1.0 / math.sqrt(3 * HEAD_DIM)
    width = c.tokens.shape[1]
    enter(links, c)
    attend(links, c, scale)
    middle(links, c)
    feed(links, c)
    end(links, c)
    feed_back(links, c)
    rings = (total(links, c.d_exp, c.exp_slots, c.exp_all, width // 2), total(links, c.d_red, c.red_slots, c.red_all, width // 2))
    step(*rings)
    middle_back(links, c, rings)

    def weights_done(low):
        def done(total):
            c.weights[:, low : low + width // 2] = total
        return done

    def tokens_done(total):
        c.d_tokens[...] = c.d_mid[...] + total

    tasks = {
        "relative": [leave_relative(links, c)],
        "grads": [ring_scatter(links, c.grads, c.grad_slots, weights_done(0), 0, width // 2, width // 2 - BLK),
                  ring_scatter(links, c.grads, c.grad_slots, weights_done(width // 2), width // 2, width, width // 2 + BLK)],
        "tokens": [group_scatter(links, c.in_part, c.in_slots, tokens_done)],
        "small": [leave_small(links, c)],
    }

    def leave(key):
        step(*tasks[key])
        if key == "grads":
            step(*tasks["relative"])

    attend_back(links, c, scale, rings, leave)
    step(*tasks["tokens"])
    finish(*tasks["relative"], *tasks["small"], *rings, *tasks["grads"], *tasks["tokens"])


def last_kernel(names, *refs):
    c = SimpleNamespace(**dict(zip(names, refs)))
    cols = c.combiner_grad.shape[1]
    c.out[...] = c.result[...]
    c.tokens_grad[...] = c.d_tokens[...]
    for m in range(3):
        c.projector_grad[m] = c.weights[:, cols * m : cols * (m + 1)]
        c.intercepts_grad[m : m + 1, :] = c.sums[BIAS : BIAS + 1, cols * m : cols * (m + 1)]
    c.combiner_grad[...] = c.weights[:, 3 * cols :]
    c.relative_grad[...] = c.rel_all[...].astype(F32)
    c.expander_grad[...] = c.exp_all[...].astype(F32)
    c.reducer_grad[...] = c.red_all[...].astype(F32)
    for key, k in (("offset", OFFSET), ("residue", RESIDUE), ("stretch", STRETCH), ("uplift", UPLIFT), ("amplify", AMPLIFY), ("displace", DISPLACE),
                   ("threshold", THRESHOLD)):
        ref = getattr(c, key + "_grad")
        ref[...] = c.sums[k : k + 1, :].reshape(ref.shape)


def shards(tokens, cotangent, selected, buckets, projector, intercepts, combiner, offset, relative, stretch, uplift,
           expander, threshold, reducer, residue, amplify, displace):
    quarter, width = tokens.shape
    cols = projector.shape[2]
    part = projector.shape[1]
    n, group = lax.axis_size("dp"), lax.axis_size("tensor")
    classes = relative.shape[0]
    length = group * quarter
    heads = cols // HEAD_DIM
    hidden = expander.shape[1]
    keep = -(-(quarter * 2 // 5) // 16) * 16
    lines = classes // group // n
    span = buckets.shape[0] + 1
    S, V = jax.ShapeDtypeStruct, pltpu.VMEM
    row = width // n
    ins = dict(tokens=tokens, cotangent=cotangent, selected=selected,
               buckets=jnp.pad(buckets, (1, 0), constant_values=-1).reshape(span // BLK, BLK),
               projector=projector, intercepts=intercepts, combiner=combiner, offset=offset, relative=relative, stretch=stretch, uplift=uplift,
               expander=expander, threshold=threshold, reducer=reducer, residue=residue, amplify=amplify, displace=displace)
    outs = dict(result=S((quarter, width), BF16), d_tokens=S((quarter, width), F32), weights=S((part, width), F32), sums=S((8, width), F32),
                rel_all=S((group, n, lines, width), BF16), exp_all=S((n, row, width), BF16), red_all=S((n, row, width), BF16))
    quarters, fews = (group, quarter, width), (group, keep, width)
    scratch = dict(
        own=V((part, width), BF16), pick=V((8, quarter), F32), x=V(quarters, BF16), w=V((n, part, width), BF16), chosen=V((group, 8, quarter), F32),
        sel=V((group, keep, quarter), BF16), probs=V((heads, length, length), F32), mixed=V((length, 3 * cols), BF16), table=V((span, 2 * cols), BF16),
        spread=V((span, classes), BF16), ctx=V((length, cols), BF16), far=V((length, length), F32), acc=V((length, cols), F32),
        part=V(quarters, BF16), part_slots=V((3, quarter, width), BF16), hidden=V(quarters, BF16), mid=V((quarter, width), F32), unit=V((quarter, width), F32),
        inverse=V((quarter, BLK), F32), feed=V(quarters, BF16), feed_slots=V((3, quarter, width), BF16), d_end=V((quarter, width), F32),
        d_rows=V(fews, BF16), small=V((8, width), F32), back=V(fews, BF16), back_slots=V((3, keep, width), BF16), d_mid=V((quarter, width), F32),
        d_attn=V(fews, BF16), d_exp=V((n, row, width), BF16), d_red=V((n, row, width), BF16), exp_slots=V((2, n // 2, row, width), BF16),
        red_slots=V((2, n // 2, row, width), BF16), dctx=V((length, cols), BF16), dctx_t=V((cols, length), BF16), turn_t=V((2 * cols, length), BF16),
        dq=V((length, cols), F32), dk=V((length, cols), F32), dv_t=V((cols, length), F32), dpos_t=V((2 * cols, span), F32), ds=V((length, length), BF16),
        grads=V((n, part, width), BF16), in_part=V(quarters, BF16), rel_part=V((group, classes // group, width), BF16),
        grad_slots=V((2, n // 2, part, width), BF16), in_slots=V((3, quarter, width), BF16), rel_slots=V((3, classes // group, width), BF16),
        rel_own=V((n, lines, width), BF16), rel_ring=V((2, n // 2, lines, width), BF16), small_all=V((n, 8, width), F32), small_slots=V((3, 8, width), F32),
        send=pltpu.SemaphoreType.DMA((11 * n + 40,)), recv=pltpu.SemaphoreType.DMA((11 * n + 40,)))
    made = pl.pallas_call(
        functools.partial(layer_kernel, n, list(ins) + list(outs) + list(scratch)),
        out_shape=tuple(outs.values()),
        scratch_shapes=list(scratch.values()),
        compiler_params=pltpu.CompilerParams(collective_id=1, has_side_effects=True),
        name="layer",
    )(*ins.values())
    kept = dict(zip(outs, made))
    kept["rel_all"] = kept["rel_all"].reshape(classes, width)
    kept["exp_all"] = kept["exp_all"].reshape(expander.shape)
    kept["red_all"] = kept["red_all"].reshape(reducer.shape)
    lasts = dict(out=S((quarter, width), BF16), tokens_grad=S((quarter, width), F32), projector_grad=S(projector.shape, F32),
                 intercepts_grad=S(intercepts.shape, F32), combiner_grad=S(combiner.shape, F32), offset_grad=S(offset.shape, F32),
                 relative_grad=S(relative.shape, F32), stretch_grad=S(stretch.shape, F32), uplift_grad=S(uplift.shape, F32),
                 expander_grad=S(expander.shape, F32), threshold_grad=S(threshold.shape, F32), reducer_grad=S(reducer.shape, F32),
                 residue_grad=S(residue.shape, F32), amplify_grad=S(amplify.shape, F32), displace_grad=S(displace.shape, F32))
    return pl.pallas_call(functools.partial(last_kernel, list(kept) + list(lasts)), out_shape=tuple(lasts.values()), name="last")(*kept.values())


def solution(mesh):
    both = P(("dp", "tensor"), None)
    return jax.shard_map(
        shards,
        mesh=mesh,
        in_specs=(both, both, P(("dp", "tensor")), P(), P(None, "dp", "tensor"), P(None, "tensor"), P("dp", "tensor"), P(), P(), P(), P(),
                  P(None, "tensor"), P("tensor"), P("tensor", None), P(), P(), P()),
        out_specs=(both, both, P(None, "dp", "tensor"), P(None, "tensor"), P("dp", "tensor"), P(), P(), P(), P(),
                   P(None, "tensor"), P("tensor"), P("tensor", None), P(), P(), P()),
        check_vma=False,
    )
```
